32 devices in a mesh: outer: 4 (over z), dev: 8 (over y, x, core).
Axes of the slice: x: 2, y: 2, z: 4, core: 2. Of those that a mesh axis runs over, the one named last changes fastest.
Arguments:
- partials: bfloat16 [32, 8192, 128], P(('outer', 'dev')), may hold values from -6 to 6
- p_old: bfloat16 [8192, 1024], P('dev'), may hold values from -0.0625 to 0.0625
- p_new: bfloat16 [8192, 1024], P('dev'), may hold values from -0.0625 to 0.0625
- weight: float32 [8192, 128], P('dev'), may hold values from -4 to 4
- m_old: float32 [1024, 128], P('dev'), may hold values from -96 to 96
- v_old: float32 [1024, 128], P('dev'), may hold values from 32 to 1280
Outputs:
- new_weight: float32 [8192, 128], P('dev')
- m_new: float32 [1024, 128], P('dev')
- v_new: float32 [1024, 128], P('dev')
The draws below stay inside these ranges and needn't reach their ends.
All inputs are finite; a program needn't handle non-finite values.
Results may differ from the reference program's by a relative error of at most 0.0012.
Values may be sent and summed in bfloat16 or wider, within the bound.
A program may use at most 128 MiB of HBM per device.

```python
import math
import jax
import jax.numpy as jnp
from jax import lax

D = 8192
R = 1024
COLS = 128
DEVICES = 32


def levels(own_key, extent, shards, smallest, top_value):
    gain, own = 1.0, jax.random.fold_in(own_key, 6)
    for axis_at, shards_of in shards:
        heights = jnp.exp(jax.random.uniform(jax.random.fold_in(own, axis_at), (shards_of,), jnp.float32, smallest / len(shards), top_value / len(shards)))
        gain = gain * jnp.repeat(heights, extent[axis_at] // shards_of).reshape([-1 if axis == axis_at else 1 for axis in range(len(extent))])
    return gain


def centred(own_key, dims, deviation, limit, split=(), held_as=jnp.bfloat16):
    values = deviation * jax.random.normal(own_key, dims, jnp.float32)
    if split:
        values = values * levels(own_key, dims, split, -0.22, 0.18)
    return jnp.clip(values, -limit, limit).astype(held_as)


def setup_inputs(seed: int = 0) -> dict:
    streams_of = jax.random.split(jax.random.key(seed), 7)
    return {
        "partials": centred(streams_of[0], (DEVICES, D, COLS), 1.0, 6.0, ((0, 32),)),
        "p_old": centred(streams_of[1], (D, R), D ** -0.5, 0.0625, ((0, 8),)),
        "p_new": centred(streams_of[2], (D, R), D ** -0.5, 0.0625, ((0, 8),)),
        "weight": centred(streams_of[3], (D, COLS), 0.3, 4.0, ((0, 8),), jnp.float32),
        "m_old": centred(streams_of[4], (R, COLS), 16.0, 96.0, ((0, 8),), jnp.float32),
        "v_old": jnp.clip(jnp.exp(math.log(1280.0) - 3.6888795 * jax.random.uniform(streams_of[5], (R, COLS), jnp.float32) ** levels(streams_of[5], (R, COLS), ((0, 8),), -0.2, 0.2)), 32.0, 1280.0),
    }


beta_mean = 0.9
beta_square = 0.95
bias_mean = 0.9999734386011124
bias_square = 0.9940794707796659
adam_epsilon = 1e-08
step_scale = 0.5

def reference(partials, p_old, p_new, weight, m_old, v_old):

    def accumulate(total, piece):
        return (total + piece.astype(jnp.float32), None)
    grad, _ = lax.scan(accumulate, jnp.zeros((D, COLS), jnp.float32), partials)
    projected = jnp.dot(p_new.astype(jnp.float32).T, grad, precision=lax.Precision.HIGHEST)
    margin = jnp.dot(p_new.T, p_old, preferred_element_type=jnp.float32)
    m_rot = jnp.dot(margin, m_old, precision=lax.Precision.HIGHEST)
    v_rot = jnp.dot(margin * margin, v_old, precision=lax.Precision.HIGHEST)
    m_new = beta_mean * m_rot + (1.0 - beta_mean) * projected
    v_new = beta_square * v_rot + (1.0 - beta_square) * projected * projected
    direction = (m_new / bias_mean / (jnp.sqrt(v_new / bias_square) + adam_epsilon)).astype(jnp.bfloat16)
    update = jnp.dot(p_new, direction, preferred_element_type=jnp.float32)
    new_weight = weight - step_scale * update
    return (new_weight, m_new, v_new)
```

```python
import functools

import jax
import jax.numpy as jnp
from jax import lax
from jax.experimental import pallas as pl
from jax.experimental.pallas import tpu as pltpu
from jax.sharding import PartitionSpec as P

beta_mean = 0.9
beta_square = 0.95
bias_mean = 0.9999734386011124
bias_square = 0.9940794707796659
adam_epsilon = 1e-08
step_scale = 0.5

MESH = pl.DeviceIdType.MESH
F32 = jnp.float32
BF16 = jnp.bfloat16


def contract_rows(a, b):
    return lax.dot_general(a, b, (((0,), (0,)), ((), ())), preferred_element_type=F32)


def kernel(
    n_outer,
    n_dev,
    partials,
    p_old,
    p_new,
    weight,
    m_old,
    v_old,
    new_weight,
    m_new,
    v_new,
    grads,
    basis,
    basis_old,
    weights,
    moments,
    margin,
    margin_partner,
    margin_sum,
    margin_in,
    rotated,
    rotated_in,
    projected,
    projected_partner,
    projected_sum,
    projected_in,
    block,
    block_in,
    direction,
    load_sem,
    grad_send,
    grad_recv,
    mom_send,
    mom_recv,
    fwd_send,
    fwd_recv,
    mp_send,
    mp_recv,
    ms_send,
    ms_recv,
    rot_send,
    rot_recv,
    pp_send,
    pp_recv,
    ps_send,
    ps_recv,
    blk_send,
    blk_recv,
    dir_send,
    dir_recv,
):
    z = lax.axis_index("outer")
    d = lax.axis_index("dev")
    n_chip = n_dev // 2
    q = d // 2
    c = d % 2
    partner = q * 2 + 1 - c
    rows, cols = weight.shape
    rank = p_new.shape[1]
    blk = rank // n_dev
    per = n_dev // n_outer

    def remote(src, dst, send, recv, where):
        return pltpu.make_async_remote_copy(
            src_ref=src, dst_ref=dst, send_sem=send, recv_sem=recv, device_id=where, device_id_type=MESH
        )

    barrier = pltpu.get_barrier_semaphore()
    for j in range(1, n_dev):
        pl.semaphore_signal(barrier, inc=1, device_id=(z, lax.rem(d + j, n_dev)), device_id_type=MESH)
    for j in range(1, n_outer):
        pl.semaphore_signal(barrier, inc=1, device_id=(lax.rem(z + j, n_outer), d), device_id_type=MESH)

    load_new = pltpu.make_async_copy(p_new, basis, load_sem.at[0])
    load_new.start()
    load_old = pltpu.make_async_copy(p_old, basis_old, load_sem.at[1])
    load_old.start()
    load_weight = pltpu.make_async_copy(weight, weights, load_sem.at[2])
    load_weight.start()
    load_own = pltpu.make_async_copy(
        partials.at[pl.ds(pl.multiple_of(d * rows, rows), rows)], grads.at[0], load_sem.at[3]
    )
    load_own.start()

    pl.semaphore_wait(barrier, n_dev - 1 + n_outer - 1)

    def moment_copies(k, owner):
        copies = []
        for j in range(1, n_chip):
            to = (z, lax.rem(q + j, n_chip) * 2 + c)
            for i, src in enumerate((m_old, v_old)):
                copies.append(remote(src, moments.at[i, k], mom_send.at[i, k, j], mom_recv.at[i, k], to))
        return copies

    for k in range(per):
        owner = z * per + k

        @pl.when(d == owner)
        def _():
            for copy in moment_copies(k, owner):
                copy.start()
            for i, src in enumerate((m_old, v_old)):
                pltpu.make_async_copy(src, moments.at[i, k], load_sem.at[4 + i]).start()

    grad_copies = []
    for j in range(1, n_dev):
        to = lax.rem(d + j, n_dev)
        copy = remote(
            partials.at[pl.ds(pl.multiple_of(to * rows, rows), rows)],
            grads.at[j],
            grad_send.at[j],
            grad_recv.at[j],
            (z, to),
        )
        copy.start()
        grad_copies.append(copy)

    load_new.wait()
    load_old.wait()
    width = min(rank, 256)
    for s in range(0, rank, width):
        part = contract_rows(basis[:, s : s + width], basis_old[...])
        margin[s // blk : (s + width) // blk] = part.reshape(width // blk, blk, part.shape[1])

    def scatter_start(val, prt, send, recv):
        copies = []
        for j in list(range(1, n_chip)) + [0]:
            k = lax.rem(q + j, n_chip)
            copy = remote(val.at[2 * k + 1 - c], prt.at[j], send.at[j], recv.at[j], (z, partner))
            copy.start()
            copies.append((j, k, copy))
        return copies

    def scatter_middle(pairs, val, prt, tot, arr, send, recv):
        copies = []
        for j, k, pair in pairs:
            pair.wait_recv()
            tot[j] = val[2 * k + c] + prt[j]
            if j:
                copy = remote(tot.at[j], arr.at[j], send.at[j], recv.at[j], (z, 2 * k + c))
                copy.start()
                copies.append((j, copy))
        return copies

    def scatter_end(copies, tot, arr):
        total = tot[0]
        for j, copy in copies:
            copy.wait_recv()
            total = total + arr[j]
        return total

    margin_pairs = scatter_start(margin, margin_partner, mp_send, mp_recv)

    for k in range(per):
        owner = z * per + k
        mine = c == owner % 2

        @pl.when(d == owner)
        def _():
            for i, src in enumerate((m_old, v_old)):
                pltpu.make_async_copy(src, moments.at[i, k], load_sem.at[4 + i]).wait()

        @pl.when(jnp.logical_and(mine, d != owner))
        def _():
            for i, src in enumerate((m_old, v_old)):
                remote(src, moments.at[i, k], mom_send.at[i, k, 0], mom_recv.at[i, k], (z, d)).wait_recv()

        @pl.when(mine)
        def _():
            for i in range(2):
                remote(
                    moments.at[i, k], moments.at[i, k], fwd_send.at[i, k], fwd_recv.at[i, k], (z, partner)
                ).start()

    margin_copies = scatter_middle(
        margin_pairs, margin, margin_partner, margin_sum, margin_in, ms_send, ms_recv
    )

    for k in range(per):
        mine = c == (z * per + k) % 2

        @pl.when(jnp.logical_not(mine))
        def _():
            for i in range(2):
                remote(
                    moments.at[i, k], moments.at[i, k], fwd_send.at[i, k], fwd_recv.at[i, k], (z, partner)
                ).wait_recv()

    margin_rows = scatter_end(margin_copies, margin_sum, margin_in)
    old = moments[...].reshape(2, per * blk, cols)
    rotated[0] = jnp.dot(margin_rows, old[0], precision=lax.Precision.HIGHEST, preferred_element_type=F32)
    rotated[1] = jnp.dot(
        margin_rows * margin_rows, old[1], precision=lax.Precision.HIGHEST, preferred_element_type=F32
    )
    rot_copies = []
    for j in range(1, n_outer):
        copy = remote(
            rotated, rotated_in.at[j], rot_send.at[j], rot_recv.at[j], (lax.rem(z + j, n_outer), d)
        )
        copy.start()
        rot_copies.append(copy)

    load_own.wait()
    for copy in grad_copies:
        copy.wait_recv()
    total = grads[0].astype(F32)
    for j in range(1, n_dev):
        total = total + grads[j].astype(F32)
    high = total.astype(BF16)
    low = (total - high.astype(F32)).astype(BF16)
    both = jnp.concatenate([high, low], axis=1)
    for s in range(0, rank, width):
        part = contract_rows(basis[:, s : s + width], both)
        part = part[:, :cols] + part[:, cols:]
        projected[s // blk : (s + width) // blk] = part.reshape(width // blk, blk, cols)
    pairs = scatter_start(projected, projected_partner, pp_send, pp_recv)
    copies = scatter_middle(
        pairs, projected, projected_partner, projected_sum, projected_in, ps_send, ps_recv
    )
    block[...] = scatter_end(copies, projected_sum, projected_in)
    blk_copies = []
    for j in range(1, n_outer):
        copy = remote(
            block, block_in.at[j], blk_send.at[j], blk_recv.at[j], (lax.rem(z + j, n_outer), d)
        )
        copy.start()
        blk_copies.append(copy)
    for copy in rot_copies:
        copy.wait_recv()
    for copy in blk_copies:
        copy.wait_recv()

    first = rotated[0]
    second = rotated[1]
    proj = block[...]
    for j in range(1, n_outer):
        first = first + rotated_in[j, 0]
        second = second + rotated_in[j, 1]
        proj = proj + block_in[j]
    mean = beta_mean * first + (1.0 - beta_mean) * proj
    square = beta_square * second + (1.0 - beta_square) * proj * proj
    m_new[...] = mean
    v_new[...] = square
    direction[d] = (mean / bias_mean / (jnp.sqrt(square / bias_square) + adam_epsilon)).astype(BF16)
    dir_copies = []
    for j in range(1, n_dev):
        copy = remote(
            direction.at[d], direction.at[d], dir_send.at[j], dir_recv.at[j], (z, lax.rem(d + j, n_dev))
        )
        copy.start()
        dir_copies.append(copy)
    load_weight.wait()
    for copy in dir_copies:
        copy.wait_recv()
    directions = direction[...].reshape(rank, cols)
    tall = min(rows, 256)
    for s in range(0, rows, tall):
        update = jnp.dot(basis[s : s + tall, :], directions, preferred_element_type=F32)
        new_weight[s : s + tall, :] = weights[s : s + tall, :] - step_scale * update

    for k in range(per):
        owner = z * per + k
        mine = c == owner % 2

        @pl.when(d == owner)
        def _():
            for copy in moment_copies(k, owner):
                copy.wait_send()

        @pl.when(mine)
        def _():
            for i in range(2):
                remote(
                    moments.at[i, k], moments.at[i, k], fwd_send.at[i, k], fwd_recv.at[i, k], (z, partner)
                ).wait_send()

    for copy in grad_copies + rot_copies + blk_copies + dir_copies:
        copy.wait_send()
    for group in (margin_pairs, pairs):
        for _, _, copy in group:
            copy.wait_send()
    for group in (margin_copies, copies):
        for _, copy in group:
            copy.wait_send()


def on_device(n_outer, n_dev, partials, p_old, p_new, weight, m_old, v_old):
    rows, cols = weight.shape
    rank = p_new.shape[1]
    blk = rank // n_dev
    per = n_dev // n_outer
    span = per * blk
    n_chip = n_dev // 2
    p_old = lax.dynamic_slice_in_dim(p_old, lax.axis_index("outer") * span, span, axis=1)
    dma = pltpu.SemaphoreType.DMA
    anywhere = pl.BlockSpec(memory_space=pl.ANY)
    vmem = pl.BlockSpec(memory_space=pltpu.VMEM)
    return pl.pallas_call(
        functools.partial(kernel, n_outer, n_dev),
        out_shape=(
            jax.ShapeDtypeStruct((rows, cols), F32),
            jax.ShapeDtypeStruct((blk, cols), F32),
            jax.ShapeDtypeStruct((blk, cols), F32),
        ),
        in_specs=[anywhere] * 6,
        out_specs=(vmem, vmem, vmem),
        scratch_shapes=[
            pltpu.VMEM((n_dev, rows, cols), BF16),
            pltpu.VMEM((rows, rank), BF16),
            pltpu.VMEM((rows, span), BF16),
            pltpu.VMEM((rows, cols), F32),
            pltpu.VMEM((2, per, blk, cols), F32),
            pltpu.VMEM((n_dev, blk, span), F32),
            pltpu.VMEM((n_chip, blk, span), F32),
            pltpu.VMEM((n_chip, blk, span), F32),
            pltpu.VMEM((n_chip, blk, span), F32),
            pltpu.VMEM((2, blk, cols), F32),
            pltpu.VMEM((n_outer, 2, blk, cols), F32),
            pltpu.VMEM((n_dev, blk, cols), F32),
            pltpu.VMEM((n_chip, blk, cols), F32),
            pltpu.VMEM((n_chip, blk, cols), F32),
            pltpu.VMEM((n_chip, blk, cols), F32),
            pltpu.VMEM((blk, cols), F32),
            pltpu.VMEM((n_outer, blk, cols), F32),
            pltpu.VMEM((n_dev, blk, cols), BF16),
            dma((6,)),
            dma((n_dev,)),
            dma((n_dev,)),
            dma((2, per, n_chip)),
            dma((2, per)),
            dma((2, per)),
            dma((2, per)),
        ]
        + [dma((n_chip,))] * 4
        + [dma((n_outer,))] * 2
        + [dma((n_chip,))] * 4
        + [dma((n_outer,))] * 2
        + [dma((n_dev,))] * 2,
        compiler_params=pltpu.CompilerParams(
            collective_id=0, has_side_effects=True, vmem_limit_bytes=48 * 1024 * 1024
        ),
    )(partials[0], p_old, p_new, weight, m_old, v_old)


def solution(mesh):
    in_specs = (
        P(("outer", "dev"), None, None),
        P("dev", None),
        P("dev", None),
        P("dev", None),
        P("dev", None),
        P("dev", None),
    )
    out_specs = (P("dev", None), P("dev", None), P("dev", None))
    return jax.shard_map(
        functools.partial(on_device, mesh.shape["outer"], mesh.shape["dev"]),
        mesh=mesh,
        in_specs=in_specs,
        out_specs=out_specs,
        check_vma=False,
    )
```

```python
import functools

import jax
import jax.numpy as jnp
from jax import lax
from jax.experimental import pallas as pl
from jax.experimental.pallas import tpu as pltpu
from jax.sharding import PartitionSpec as P

beta_mean = 0.9
beta_square = 0.95
bias_mean = 0.9999734386011124
bias_square = 0.9940794707796659
adam_epsilon = 1e-08
step_scale = 0.5

chunks = 2
vmem_limit = 67043328
finish_limit = 67043328

MESH = pl.DeviceIdType.MESH
F32 = jnp.float32
BF16 = jnp.bfloat16


def contract_rows(a, b):
    return lax.dot_general(a, b, (((0,), (0,)), ((), ())), preferred_element_type=F32)


def kernel(
    n_outer,
    n_dev,
    partials,
    p_old,
    p_new,
    weight,
    m_old,
    v_old,
    new_weight,
    m_new,
    v_new,
    grads,
    basis,
    basis_old,
    weights,
    moments,
    margin,
    margin_partner,
    margin_sum,
    margin_in,
    rotated,
    rotated_in,
    projected,
    projected_partner,
    projected_sum,
    projected_in,
    block,
    block_in,
    direction,
    load_sem,
    old_sem,
    grad_send,
    grad_recv,
    mom_send,
    mom_recv,
    fwd_send,
    fwd_recv,
    mp_send,
    mp_recv,
    ms_send,
    ms_recv,
    rot_send,
    rot_recv,
    pp_send,
    pp_recv,
    ps_send,
    ps_recv,
    blk_send,
    blk_recv,
    dir_send,
    dir_recv,
):
    z = lax.axis_index("outer")
    d = lax.axis_index("dev")
    n_chip = n_dev // 2
    q = d // 2
    c = d % 2
    partner = q * 2 + 1 - c
    rows, cols = weight.shape
    rank = p_new.shape[1]
    blk = rank // n_dev
    per = n_dev // n_outer

    def remote(src, dst, send, recv, where):
        return pltpu.make_async_remote_copy(
            src_ref=src, dst_ref=dst, send_sem=send, recv_sem=recv, device_id=where, device_id_type=MESH
        )

    barrier = pltpu.get_barrier_semaphore()
    for j in range(1, n_dev):
        pl.semaphore_signal(barrier, inc=1, device_id=(z, lax.rem(d + j, n_dev)), device_id_type=MESH)
    for j in range(1, n_outer):
        pl.semaphore_signal(barrier, inc=1, device_id=(lax.rem(z + j, n_outer), d), device_id_type=MESH)

    load_new = pltpu.make_async_copy(p_new, basis, load_sem.at[0])
    load_new.start()
    if p_old.shape[1] == per * blk:
        old_loads = [pltpu.make_async_copy(p_old, basis_old, old_sem.at[0])]
    else:
        old_loads = [
            pltpu.make_async_copy(
                p_old.at[:, pl.ds(pl.multiple_of((k * n_outer + z) * blk, blk), blk)],
                basis_old.at[:, k * blk : (k + 1) * blk],
                old_sem.at[k],
            )
            for k in range(per)
        ]
    for load in old_loads:
        load.start()
    load_weight = pltpu.make_async_copy(weight, weights, load_sem.at[2])
    load_weight.start()
    load_own = pltpu.make_async_copy(
        partials.at[pl.ds(pl.multiple_of(d * rows, rows), rows)], grads.at[0], load_sem.at[3]
    )
    load_own.start()

    pl.semaphore_wait(barrier, n_dev - 1 + n_outer - 1)

    def moment_copies(k, owner):
        copies = []
        for j in range(1, n_chip):
            to = (z, lax.rem(q + j, n_chip) * 2 + c)
            for i, src in enumerate((m_old, v_old)):
                copies.append(remote(src, moments.at[i, k], mom_send.at[i, k, j], mom_recv.at[i, k], to))
        return copies

    for k in range(per):
        owner = k * n_outer + z

        @pl.when(d == owner)
        def _():
            for copy in moment_copies(k, owner):
                copy.start()
            for i, src in enumerate((m_old, v_old)):
                pltpu.make_async_copy(src, moments.at[i, k], load_sem.at[4 + i]).start()

    tall = rows // chunks

    def send_gradients(chunk):
        copies = []
        for j in range(1, n_dev):
            to = lax.rem(d + j, n_dev)
            copy = remote(
                partials.at[pl.ds(pl.multiple_of(to * rows + chunk * tall, tall), tall)],
                grads.at[j, chunk * tall : (chunk + 1) * tall],
                grad_send.at[chunk, j],
                grad_recv.at[chunk, j],
                (z, to),
            )
            copy.start()
            copies.append(copy)
        return copies

    grad_copies = [send_gradients(0)]

    load_new.wait()
    for load in old_loads:
        load.wait()
    width = min(rank, 256)
    for s in range(0, rank, width):
        part = contract_rows(basis[:, s : s + width], basis_old[...])
        margin[s // blk : (s + width) // blk] = part.reshape(width // blk, blk, part.shape[1])

    def scatter_start(val, prt, send, recv):
        copies = []
        for j in list(range(1, n_chip)) + [0]:
            k = lax.rem(q + j, n_chip)
            copy = remote(val.at[2 * k + 1 - c], prt.at[j], send.at[j], recv.at[j], (z, partner))
            copy.start()
            copies.append((j, k, copy))
        return copies

    def scatter_middle(pairs, val, prt, tot, arr, send, recv):
        copies = []
        for j, k, pair in pairs:
            pair.wait_recv()
            tot[j] = val[2 * k + c] + prt[j]
            if j:
                copy = remote(tot.at[j], arr.at[j], send.at[j], recv.at[j], (z, 2 * k + c))
                copy.start()
                copies.append((j, copy))
        return copies

    def scatter_end(copies, tot, arr):
        total = tot[0]
        for j, copy in copies:
            copy.wait_recv()
            total = total + arr[j]
        return total

    margin_pairs = scatter_start(margin, margin_partner, mp_send, mp_recv)

    for k in range(per):
        owner = k * n_outer + z
        mine = c == owner % 2

        @pl.when(d == owner)
        def _():
            for i, src in enumerate((m_old, v_old)):
                pltpu.make_async_copy(src, moments.at[i, k], load_sem.at[4 + i]).wait()

        @pl.when(jnp.logical_and(mine, d != owner))
        def _():
            for i, src in enumerate((m_old, v_old)):
                remote(src, moments.at[i, k], mom_send.at[i, k, 0], mom_recv.at[i, k], (z, d)).wait_recv()

        @pl.when(mine)
        def _():
            for i in range(2):
                remote(
                    moments.at[i, k], moments.at[i, k], fwd_send.at[i, k], fwd_recv.at[i, k], (z, partner)
                ).start()

    margin_copies = scatter_middle(
        margin_pairs, margin, margin_partner, margin_sum, margin_in, ms_send, ms_recv
    )

    for chunk in range(1, chunks):
        grad_copies.append(send_gradients(chunk))

    for k in range(per):
        mine = c == (k * n_outer + z) % 2

        @pl.when(jnp.logical_not(mine))
        def _():
            for i in range(2):
                remote(
                    moments.at[i, k], moments.at[i, k], fwd_send.at[i, k], fwd_recv.at[i, k], (z, partner)
                ).wait_recv()

    margin_rows = scatter_end(margin_copies, margin_sum, margin_in)
    old = moments[...].reshape(2, per * blk, cols)
    rotated[0] = jnp.dot(margin_rows, old[0], precision=lax.Precision.HIGHEST, preferred_element_type=F32)
    rotated[1] = jnp.dot(
        margin_rows * margin_rows, old[1], precision=lax.Precision.HIGHEST, preferred_element_type=F32
    )
    rot_copies = []
    for j in range(1, n_outer):
        copy = remote(
            rotated, rotated_in.at[j], rot_send.at[j], rot_recv.at[j], (lax.rem(z + j, n_outer), d)
        )
        copy.start()
        rot_copies.append(copy)

    load_own.wait()
    for chunk in range(chunks):
        for copy in grad_copies[chunk]:
            copy.wait_recv()
        part_rows = slice(chunk * tall, (chunk + 1) * tall)
        total = grads[0, part_rows].astype(F32)
        for j in range(1, n_dev):
            total = total + grads[j, part_rows].astype(F32)
        high = total.astype(BF16)
        low = (total - high.astype(F32)).astype(BF16)
        both = jnp.concatenate([high, low], axis=1)
        for s in range(0, rank, width):
            part = contract_rows(basis[part_rows, s : s + width], both)
            part = (part[:, :cols] + part[:, cols:]).reshape(width // blk, blk, cols)
            blocks = slice(s // blk, (s + width) // blk)
            projected[blocks] = part if chunk == 0 else projected[blocks] + part
    pairs = scatter_start(projected, projected_partner, pp_send, pp_recv)
    copies = scatter_middle(
        pairs, projected, projected_partner, projected_sum, projected_in, ps_send, ps_recv
    )
    block[...] = scatter_end(copies, projected_sum, projected_in)
    blk_copies = []
    for j in range(1, n_outer):
        copy = remote(
            block, block_in.at[j], blk_send.at[j], blk_recv.at[j], (lax.rem(z + j, n_outer), d)
        )
        copy.start()
        blk_copies.append(copy)
    for copy in rot_copies:
        copy.wait_recv()
    for copy in blk_copies:
        copy.wait_recv()

    first = rotated[0]
    second = rotated[1]
    proj = block[...]
    for j in range(1, n_outer):
        first = first + rotated_in[j, 0]
        second = second + rotated_in[j, 1]
        proj = proj + block_in[j]
    mean = beta_mean * first + (1.0 - beta_mean) * proj
    square = beta_square * second + (1.0 - beta_square) * proj * proj
    m_new[...] = mean
    v_new[...] = square
    direction[d] = (mean / bias_mean / (jnp.sqrt(square / bias_square) + adam_epsilon)).astype(BF16)
    dir_copies = []
    for j in range(1, n_dev):
        copy = remote(
            direction.at[d], direction.at[d], dir_send.at[j], dir_recv.at[j], (z, lax.rem(d + j, n_dev))
        )
        copy.start()
        dir_copies.append(copy)
    load_weight.wait()
    for copy in dir_copies:
        copy.wait_recv()
    directions = direction[...].reshape(rank, cols)
    tall = min(rows, 256)
    for s in range(0, rows, tall):
        update = jnp.dot(basis[s : s + tall, :], directions, preferred_element_type=F32)
        new_weight[s : s + tall, :] = weights[s : s + tall, :] - step_scale * update

    for k in range(per):
        owner = k * n_outer + z
        mine = c == owner % 2

        @pl.when(d == owner)
        def _():
            for copy in moment_copies(k, owner):
                copy.wait_send()

        @pl.when(mine)
        def _():
            for i in range(2):
                remote(
                    moments.at[i, k], moments.at[i, k], fwd_send.at[i, k], fwd_recv.at[i, k], (z, partner)
                ).wait_send()

    for copy in sum(grad_copies, []) + rot_copies + blk_copies + dir_copies:
        copy.wait_send()
    for group in (margin_pairs, pairs):
        for _, _, copy in group:
            copy.wait_send()
    for group in (margin_copies, copies):
        for _, copy in group:
            copy.wait_send()


def hand_over(weight_in, m_in, v_in, weight_out, m_out, v_out):
    weight_out[...] = weight_in[...]
    m_out[...] = m_in[...]
    v_out[...] = v_in[...]


def on_device(n_outer, n_dev, partials, p_old, p_new, weight, m_old, v_old):
    rows, cols = weight.shape
    rank = p_new.shape[1]
    blk = rank // n_dev
    per = n_dev // n_outer
    span = per * blk
    n_chip = n_dev // 2
    if blk % 128:
        z = lax.axis_index("outer")
        p_old = jnp.concatenate(
            [
                lax.dynamic_slice_in_dim(p_old, (k * n_outer + z) * blk, blk, axis=1)
                for k in range(per)
            ],
            axis=1,
        )
    dma = pltpu.SemaphoreType.DMA
    anywhere = pl.BlockSpec(memory_space=pltpu.HBM)
    vmem = pl.BlockSpec(memory_space=pltpu.VMEM)
    results = pl.pallas_call(
        functools.partial(kernel, n_outer, n_dev),
        out_shape=(
            jax.ShapeDtypeStruct((rows, cols), F32),
            jax.ShapeDtypeStruct((blk, cols), F32),
            jax.ShapeDtypeStruct((blk, cols), F32),
        ),
        in_specs=[anywhere] * 6,
        out_specs=(vmem, vmem, vmem),
        scratch_shapes=[
            pltpu.VMEM((n_dev, rows, cols), BF16),
            pltpu.VMEM((rows, rank), BF16),
            pltpu.VMEM((rows, span), BF16),
            pltpu.VMEM((rows, cols), F32),
            pltpu.VMEM((2, per, blk, cols), F32),
            pltpu.VMEM((n_dev, blk, span), F32),
            pltpu.VMEM((n_chip, blk, span), F32),
            pltpu.VMEM((n_chip, blk, span), F32),
            pltpu.VMEM((n_chip, blk, span), F32),
            pltpu.VMEM((2, blk, cols), F32),
            pltpu.VMEM((n_outer, 2, blk, cols), F32),
            pltpu.VMEM((n_dev, blk, cols), F32),
            pltpu.VMEM((n_chip, blk, cols), F32),
            pltpu.VMEM((n_chip, blk, cols), F32),
            pltpu.VMEM((n_chip, blk, cols), F32),
            pltpu.VMEM((blk, cols), F32),
            pltpu.VMEM((n_outer, blk, cols), F32),
            pltpu.VMEM((n_dev, blk, cols), BF16),
            dma((6,)),
            dma((per,)),
            dma((chunks, n_dev)),
            dma((chunks, n_dev)),
            dma((2, per, n_chip)),
            dma((2, per)),
            dma((2, per)),
            dma((2, per)),
        ]
        + [dma((n_chip,))] * 4
        + [dma((n_outer,))] * 2
        + [dma((n_chip,))] * 4
        + [dma((n_outer,))] * 2
        + [dma((n_dev,))] * 2,
        compiler_params=pltpu.CompilerParams(
            collective_id=0, has_side_effects=True, vmem_limit_bytes=vmem_limit
        ),
    )(partials[0], p_old, p_new, weight, m_old, v_old)
    return pl.pallas_call(
        hand_over,
        out_shape=tuple(jax.ShapeDtypeStruct(r.shape, r.dtype) for r in results),
        in_specs=[vmem] * 3,
        out_specs=(vmem,) * 3,
        compiler_params=pltpu.CompilerParams(vmem_limit_bytes=finish_limit),
    )(*results)


def solution(mesh):
    in_specs = (
        P(("outer", "dev"), None, None),
        P("dev", None),
        P("dev", None),
        P("dev", None),
        P("dev", None),
        P("dev", None),
    )
    out_specs = (P("dev", None), P("dev", None), P("dev", None))
    return jax.shard_map(
        functools.partial(on_device, mesh.shape["outer"], mesh.shape["dev"]),
        mesh=mesh,
        in_specs=in_specs,
        out_specs=out_specs,
        check_vma=False,
    )
```

```python
import functools

import jax
import jax.numpy as jnp
from jax import lax
from jax.experimental import pallas as pl
from jax.experimental.pallas import tpu as pltpu
from jax.sharding import PartitionSpec as P

beta_mean = 0.9
beta_square = 0.95
bias_mean = 0.9999734386011124
bias_square = 0.9940794707796659
adam_epsilon = 1e-08
step_scale = 0.5

chunks = 2
early = 1
parts = 2
vmem_limit = 67043328
finish_limit = 67043328

MESH = pl.DeviceIdType.MESH
F32 = jnp.float32
BF16 = jnp.bfloat16


def contract_rows(a, b):
    return lax.dot_general(a, b, (((0,), (0,)), ((), ())), preferred_element_type=F32)


def kernel(
    n_outer,
    n_dev,
    partials,
    p_old,
    p_new,
    weight,
    m_old,
    v_old,
    new_weight,
    m_new,
    v_new,
    grads,
    basis,
    basis_old,
    weights,
    moments,
    margin,
    margin_partner,
    margin_sum,
    margin_in,
    rotated,
    rotated_in,
    projected,
    projected_partner,
    projected_sum,
    projected_in,
    block,
    block_in,
    direction,
    load_sem,
    old_sem,
    grad_send,
    grad_recv,
    mom_send,
    mom_recv,
    fwd_send,
    fwd_recv,
    mp_send,
    mp_recv,
    ms_send,
    ms_recv,
    rot_send,
    rot_recv,
    pp_send,
    pp_recv,
    ps_send,
    ps_recv,
    blk_send,
    blk_recv,
    dir_send,
    dir_recv,
    own_terms,
    pair_terms,
    far_sum,
    relay_in,
    merged,
    merged_in,
    own_sem,
    hop_send,
    hop_recv,
):
    z = lax.axis_index("outer")
    d = lax.axis_index("dev")
    n_chip = n_dev // 2
    q = d // 2
    c = d % 2
    partner = q * 2 + 1 - c
    rows, cols = weight.shape
    rank = p_new.shape[1]
    blk = rank // n_dev
    per = n_dev // n_outer

    def remote(src, dst, send, recv, where):
        return pltpu.make_async_remote_copy(
            src_ref=src, dst_ref=dst, send_sem=send, recv_sem=recv, device_id=where, device_id_type=MESH
        )

    barrier = pltpu.get_barrier_semaphore()
    for j in range(1, n_dev):
        pl.semaphore_signal(barrier, inc=1, device_id=(z, lax.rem(d + j, n_dev)), device_id_type=MESH)
    for j in range(1, n_outer):
        pl.semaphore_signal(barrier, inc=1, device_id=(lax.rem(z + j, n_outer), d), device_id_type=MESH)

    load_new = pltpu.make_async_copy(p_new, basis, load_sem.at[0])
    load_new.start()
    if p_old.shape[1] == per * blk:
        old_loads = [pltpu.make_async_copy(p_old, basis_old, old_sem.at[0])]
    else:
        old_loads = [
            pltpu.make_async_copy(
                p_old.at[:, pl.ds(pl.multiple_of((k * n_outer + z) * blk, blk), blk)],
                basis_old.at[:, k * blk : (k + 1) * blk],
                old_sem.at[k],
            )
            for k in range(per)
        ]
    for load in old_loads:
        load.start()
    load_weight = pltpu.make_async_copy(weight, weights, load_sem.at[2])
    load_weight.start()
    load_own = pltpu.make_async_copy(
        partials.at[pl.ds(pl.multiple_of(d * rows, rows), rows)], grads.at[0], load_sem.at[3]
    )
    load_own.start()

    pl.semaphore_wait(barrier, n_dev - 1 + n_outer - 1)

    def moment_copies(k, owner):
        copies = []
        for j in range(1, n_chip):
            to = (z, lax.rem(q + j, n_chip) * 2 + c)
            for i, src in enumerate((m_old, v_old)):
                copies.append(remote(src, moments.at[i, k], mom_send.at[i, k, j], mom_recv.at[i, k], to))
        return copies

    for k in range(per):
        owner = k * n_outer + z

        @pl.when(d == owner)
        def _():
            for copy in moment_copies(k, owner):
                copy.start()
            for i, src in enumerate((m_old, v_old)):
                pltpu.make_async_copy(src, moments.at[i, k], load_sem.at[4 + i]).start()

    tall = rows // chunks

    def send_gradients(chunk):
        copies = []
        for j in range(1, n_dev):
            to = lax.rem(d + j, n_dev)
            copy = remote(
                partials.at[pl.ds(pl.multiple_of(to * rows + chunk * tall, tall), tall)],
                grads.at[j, chunk * tall : (chunk + 1) * tall],
                grad_send.at[chunk, j],
                grad_recv.at[chunk, j],
                (z, to),
            )
            copy.start()
            copies.append(copy)
        return copies

    relayed = n_chip == 4
    hop_copies = []

    def hop(i, src, dst, to):
        copy = remote(src, dst, hop_send.at[i], hop_recv.at[i], (z, to))
        copy.start()
        hop_copies.append(copy)
        return copy

    def rows_of(to, offset, count):
        return partials.at[pl.ds(pl.multiple_of(to * rows + offset, tall), count)]

    if relayed:
        side = q + 1 - 2 * (q % 2)
        over = lax.rem(q + 2, 4)
        far = lax.rem(side + 2, 4)
        regions = ((far, 0, rows, 0), (over, 0, tall, rows), (side, tall, tall, rows + tall))
        pair_copies, own_loads = [], []
        for i, (chip, offset, count, place) in enumerate(regions):
            at = slice(place, place + count)
            pair_copies.append(hop(i, rows_of(2 * chip + 1 - c, offset, count), pair_terms.at[at], partner))
            load = pltpu.make_async_copy(
                rows_of(2 * chip + c, offset, count), own_terms.at[at], own_sem.at[i]
            )
            load.start()
            own_loads.append(load)
        direct = []
        for h, chip in enumerate((side, over)):
            at = slice(h * tall, (h + 1) * tall)
            for r in range(2):
                to = 2 * chip + (c if r == 0 else 1 - c)
                direct.append(hop(3 + 2 * h + r, rows_of(to, h * tall, tall), grads.at[2 + r, at], to))
        near = hop(7, rows_of(partner, 0, rows), grads.at[1], partner)
        pair_copies[0].wait_recv()
        own_loads[0].wait()
        far_sum[...] = own_terms[:rows].astype(F32) + pair_terms[:rows].astype(F32)
        relays = [
            hop(8 + h, far_sum.at[h * tall : (h + 1) * tall], relay_in.at[h], 2 * chip + c)
            for h, chip in enumerate((side, over))
        ]
        grad_copies = []
    else:
        grad_copies = [send_gradients(chunk) for chunk in range(early)]

    load_new.wait()
    for load in old_loads:
        load.wait()
    width = min(rank, 256)
    for s in range(0, rank, width):
        part = contract_rows(basis[:, s : s + width], basis_old[...])
        margin[s // blk : (s + width) // blk] = part.reshape(width // blk, blk, part.shape[1])

    def scatter_start(val, prt, send, recv):
        copies = []
        for j in list(range(1, n_chip)) + [0]:
            k = lax.rem(q + j, n_chip)
            copy = remote(val.at[2 * k + 1 - c], prt.at[j], send.at[j], recv.at[j], (z, partner))
            copy.start()
            copies.append((j, k, copy))
        return copies

    def scatter_middle(pairs, val, prt, tot, arr, send, recv):
        copies = []
        for j, k, pair in pairs:
            pair.wait_recv()
            tot[j] = val[2 * k + c] + prt[j]
            if j:
                copy = remote(tot.at[j], arr.at[j], send.at[j], recv.at[j], (z, 2 * k + c))
                copy.start()
                copies.append((j, copy))
        return copies

    def scatter_end(copies, tot, arr):
        total = tot[0]
        for j, copy in copies:
            copy.wait_recv()
            total = total + arr[j]
        return total

    margin_pairs = scatter_start(margin, margin_partner, mp_send, mp_recv)

    for k in range(per):
        owner = k * n_outer + z
        mine = c == owner % 2

        @pl.when(d == owner)
        def _():
            for i, src in enumerate((m_old, v_old)):
                pltpu.make_async_copy(src, moments.at[i, k], load_sem.at[4 + i]).wait()

        @pl.when(jnp.logical_and(mine, d != owner))
        def _():
            for i, src in enumerate((m_old, v_old)):
                remote(src, moments.at[i, k], mom_send.at[i, k, 0], mom_recv.at[i, k], (z, d)).wait_recv()

        @pl.when(mine)
        def _():
            for i in range(2):
                remote(
                    moments.at[i, k], moments.at[i, k], fwd_send.at[i, k], fwd_recv.at[i, k], (z, partner)
                ).start()

    margin_copies = scatter_middle(
        margin_pairs, margin, margin_partner, margin_sum, margin_in, ms_send, ms_recv
    )

    if relayed:
        passed = []
        for h, chip in enumerate((over, side)):
            at = slice(rows + h * tall, rows + (h + 1) * tall)
            pair_copies[1 + h].wait_recv()
            own_loads[1 + h].wait()
            relays[h].wait_recv()
            merged[h] = own_terms[at].astype(F32) + pair_terms[at].astype(F32) + relay_in[h]
            passed.append(hop(10 + h, merged.at[h], merged_in.at[h], 2 * chip + c))
    else:
        for chunk in range(early, chunks):
            grad_copies.append(send_gradients(chunk))

    for k in range(per):
        mine = c == (k * n_outer + z) % 2

        @pl.when(jnp.logical_not(mine))
        def _():
            for i in range(2):
                remote(
                    moments.at[i, k], moments.at[i, k], fwd_send.at[i, k], fwd_recv.at[i, k], (z, partner)
                ).wait_recv()

    margin_rows = scatter_end(margin_copies, margin_sum, margin_in)
    old = moments[...].reshape(2, per * blk, cols)
    rotated[0] = jnp.dot(margin_rows, old[0], precision=lax.Precision.HIGHEST, preferred_element_type=F32)
    rotated[1] = jnp.dot(
        margin_rows * margin_rows, old[1], precision=lax.Precision.HIGHEST, preferred_element_type=F32
    )
    rot_copies = []
    for j in range(1, n_outer):
        copy = remote(
            rotated, rotated_in.at[j], rot_send.at[j], rot_recv.at[j], (lax.rem(z + j, n_outer), d)
        )
        copy.start()
        rot_copies.append(copy)

    load_own.wait()
    for chunk in range(chunks):
        if relayed:
            if chunk == 0:
                near.wait_recv()
            for copy in direct[2 * chunk : 2 * chunk + 2] + [passed[chunk]]:
                copy.wait_recv()
        else:
            for copy in grad_copies[chunk]:
                copy.wait_recv()
        part_rows = slice(chunk * tall, (chunk + 1) * tall)
        total = grads[0, part_rows].astype(F32)
        for j in range(1, 4 if relayed else n_dev):
            total = total + grads[j, part_rows].astype(F32)
        if relayed:
            total = total + merged_in[chunk]
        high = total.astype(BF16)
        low = (total - high.astype(F32)).astype(BF16)
        both = jnp.concatenate([high, low], axis=1)
        for s in range(0, rank, width):
            part = contract_rows(basis[part_rows, s : s + width], both)
            part = (part[:, :cols] + part[:, cols:]).reshape(width // blk, blk, cols)
            blocks = slice(s // blk, (s + width) // blk)
            projected[blocks] = part if chunk == 0 else projected[blocks] + part
    half = blk // parts
    views = [slice(h * half, (h + 1) * half) for h in range(parts)]
    pairs = [
        scatter_start(projected.at[:, v], projected_partner.at[:, v], pp_send.at[h], pp_recv.at[h])
        for h, v in enumerate(views)
    ]
    copies = [
        scatter_middle(
            pairs[h],
            projected.at[:, v],
            projected_partner.at[:, v],
            projected_sum.at[:, v],
            projected_in.at[:, v],
            ps_send.at[h],
            ps_recv.at[h],
        )
        for h, v in enumerate(views)
    ]
    blk_copies = []
    for h, v in enumerate(views):
        block[v] = scatter_end(copies[h], projected_sum.at[:, v], projected_in.at[:, v])
        for j in range(1, n_outer):
            copy = remote(
                block.at[v],
                block_in.at[j, v],
                blk_send.at[h, j],
                blk_recv.at[h, j],
                (lax.rem(z + j, n_outer), d),
            )
            copy.start()
            blk_copies.append(copy)
    for copy in rot_copies:
        copy.wait_recv()
    dir_copies = []
    for h, v in enumerate(views):
        for copy in blk_copies[h * (n_outer - 1) : (h + 1) * (n_outer - 1)]:
            copy.wait_recv()
        first = rotated[0, v]
        second = rotated[1, v]
        proj = block[v]
        for j in range(1, n_outer):
            first = first + rotated_in[j, 0, v]
            second = second + rotated_in[j, 1, v]
            proj = proj + block_in[j, v]
        mean = beta_mean * first + (1.0 - beta_mean) * proj
        square = beta_square * second + (1.0 - beta_square) * proj * proj
        m_new[v] = mean
        v_new[v] = square
        direction[d, v] = (mean / bias_mean / (jnp.sqrt(square / bias_square) + adam_epsilon)).astype(BF16)
        for j in range(1, n_dev):
            copy = remote(
                direction.at[d, v],
                direction.at[d, v],
                dir_send.at[h, j],
                dir_recv.at[h, j],
                (z, lax.rem(d + j, n_dev)),
            )
            copy.start()
            dir_copies.append(copy)
    load_weight.wait()
    for copy in dir_copies:
        copy.wait_recv()
    directions = direction[...].reshape(rank, cols)
    tall = min(rows, 256)
    for s in range(0, rows, tall):
        update = jnp.dot(basis[s : s + tall, :], directions, preferred_element_type=F32)
        new_weight[s : s + tall, :] = weights[s : s + tall, :] - step_scale * update

    for k in range(per):
        owner = k * n_outer + z
        mine = c == owner % 2

        @pl.when(d == owner)
        def _():
            for copy in moment_copies(k, owner):
                copy.wait_send()

        @pl.when(mine)
        def _():
            for i in range(2):
                remote(
                    moments.at[i, k], moments.at[i, k], fwd_send.at[i, k], fwd_recv.at[i, k], (z, partner)
                ).wait_send()

    for copy in hop_copies + sum(grad_copies, []) + rot_copies + blk_copies + dir_copies:
        copy.wait_send()
    for group in [margin_pairs] + pairs:
        for _, _, copy in group:
            copy.wait_send()
    for group in [margin_copies] + copies:
        for _, copy in group:
            copy.wait_send()


def hand_over(weight_in, m_in, v_in, weight_out, m_out, v_out):
    weight_out[...] = weight_in[...]
    m_out[...] = m_in[...]
    v_out[...] = v_in[...]


def on_device(n_outer, n_dev, partials, p_old, p_new, weight, m_old, v_old):
    rows, cols = weight.shape
    rank = p_new.shape[1]
    blk = rank // n_dev
    per = n_dev // n_outer
    span = per * blk
    n_chip = n_dev // 2
    if blk % 128:
        z = lax.axis_index("outer")
        p_old = jnp.concatenate(
            [
                lax.dynamic_slice_in_dim(p_old, (k * n_outer + z) * blk, blk, axis=1)
                for k in range(per)
            ],
            axis=1,
        )
    dma = pltpu.SemaphoreType.DMA
    anywhere = pl.BlockSpec(memory_space=pltpu.HBM)
    vmem = pl.BlockSpec(memory_space=pltpu.VMEM)
    results = pl.pallas_call(
        functools.partial(kernel, n_outer, n_dev),
        out_shape=(
            jax.ShapeDtypeStruct((rows, cols), F32),
            jax.ShapeDtypeStruct((blk, cols), F32),
            jax.ShapeDtypeStruct((blk, cols), F32),
        ),
        in_specs=[anywhere] * 6,
        out_specs=(vmem, vmem, vmem),
        scratch_shapes=[
            pltpu.VMEM((n_dev, rows, cols), BF16),
            pltpu.VMEM((rows, rank), BF16),
            pltpu.VMEM((rows, span), BF16),
            pltpu.VMEM((rows, cols), F32),
            pltpu.VMEM((2, per, blk, cols), F32),
            pltpu.VMEM((n_dev, blk, span), F32),
            pltpu.VMEM((n_chip, blk, span), F32),
            pltpu.VMEM((n_chip, blk, span), F32),
            pltpu.VMEM((n_chip, blk, span), F32),
            pltpu.VMEM((2, blk, cols), F32),
            pltpu.VMEM((n_outer, 2, blk, cols), F32),
            pltpu.VMEM((n_dev, blk, cols), F32),
            pltpu.VMEM((n_chip, blk, cols), F32),
            pltpu.VMEM((n_chip, blk, cols), F32),
            pltpu.VMEM((n_chip, blk, cols), F32),
            pltpu.VMEM((blk, cols), F32),
            pltpu.VMEM((n_outer, blk, cols), F32),
            pltpu.VMEM((n_dev, blk, cols), BF16),
            dma((6,)),
            dma((per,)),
            dma((chunks, n_dev)),
            dma((chunks, n_dev)),
            dma((2, per, n_chip)),
            dma((2, per)),
            dma((2, per)),
            dma((2, per)),
        ]
        + [dma((n_chip,))] * 4
        + [dma((n_outer,))] * 2
        + [dma((parts, n_chip))] * 4
        + [dma((parts, n_outer))] * 2
        + [dma((parts, n_dev))] * 2
        + [
            pltpu.VMEM((2 * rows, cols), BF16),
            pltpu.VMEM((2 * rows, cols), BF16),
            pltpu.VMEM((rows, cols), F32),
            pltpu.VMEM((2, rows // 2, cols), F32),
            pltpu.VMEM((2, rows // 2, cols), F32),
            pltpu.VMEM((2, rows // 2, cols), F32),
            dma((3,)),
            dma((12,)),
            dma((12,)),
        ],
        compiler_params=pltpu.CompilerParams(
            collective_id=0, has_side_effects=True, vmem_limit_bytes=vmem_limit
        ),
    )(partials[0], p_old, p_new, weight, m_old, v_old)
    return pl.pallas_call(
        hand_over,
        out_shape=tuple(jax.ShapeDtypeStruct(r.shape, r.dtype) for r in results),
        in_specs=[vmem] * 3,
        out_specs=(vmem,) * 3,
        compiler_params=pltpu.CompilerParams(vmem_limit_bytes=finish_limit),
    )(*results)


def solution(mesh):
    in_specs = (
        P(("outer", "dev"), None, None),
        P("dev", None),
        P("dev", None),
        P("dev", None),
        P("dev", None),
        P("dev", None),
    )
    out_specs = (P("dev", None), P("dev", None), P("dev", None))
    return jax.shard_map(
        functools.partial(on_device, mesh.shape["outer"], mesh.shape["dev"]),
        mesh=mesh,
        in_specs=in_specs,
        out_specs=out_specs,
        check_vma=False,
    )
```
